768 devices in a mesh: img: 48 (over y_lo, z, core), txt: 16 (over x, y_hi).
Axes of the slice: x: 4, y: 8 (y_hi: 4, y_lo: 2; y = y_hi * 2 + y_lo), z: 12, core: 2. Of those that a mesh axis runs over, the one named last changes fastest.
Arguments:
- image_emb: float32 [6144, 1536], P('img', 'txt'), may hold values from -0.15625 to 0.15625
- text_emb: float32 [6144, 1536], P('txt', 'img'), may hold values from -0.15625 to 0.15625
- vision_feat: bfloat16 [6144, 5120], P('img', 'txt'), may hold values from -0.125 to 0.125
- positive: int32 [6144], P('img'), may hold values from 0 to 6143, each once
- logit_scale: float32 [1], replicated, may hold values from 5 to 15
- logit_bias: float32 [1], replicated, may hold values from -3 to -1
Outputs:
- grad_image: float32 [6144, 1536], P('img', 'txt')
- grad_text: float32 [6144, 1536], P('txt', 'img')
- grad_proj: float32 [5120, 1536], P('txt', 'img')
The draws below stay inside these ranges and needn't reach their ends.
Inputs may be any that keep to these rules, and one draw needn't show every extreme that they name: `positive`: each text index is the match of exactly one image.
All inputs are finite; a program needn't handle non-finite values.
Results may differ from the reference program's by a relative error of at most 0.0029.
Values may be sent and summed in bfloat16 or wider, within the bound.
No kernel may reach another device: no remote copies, remote signals or barrier semaphores. Data moves between devices by JAX's collectives and lax.ppermute only.
A program may use at most 32 MiB of HBM per device.

```python
import jax
import jax.numpy as jnp
from jax import lax

EMB = 1536
VIS = 5120
ROWS_IMG = 128
PAIRS = 6144
N_IMG = 48


def block_levels(key, shape, cuts, low, high):
    def one(dim, parts):
        draws = jax.random.uniform(jax.random.fold_in(jax.random.fold_in(key, 6), dim), (parts,), jnp.float32, low / len(cuts), high / len(cuts))
        return jnp.repeat(jnp.exp(draws), shape[dim] // parts).reshape((-1,) + (1,) * (len(shape) - dim - 1))

    loudness = one(*cuts[0])
    for cut in cuts[1:]:
        loudness = loudness * one(*cut)
    return loudness


def normal_values(rng, extent, deviation, most, cuts=(), kind=jnp.bfloat16):
    values = deviation * jax.random.normal(rng, extent, jnp.float32)
    if cuts:
        values = values * block_levels(rng, extent, cuts, -0.22, 0.18)
    return jnp.clip(values, -most, most).astype(kind)


def setup_inputs(seed: int = 0) -> dict:
    arg_keys = jax.random.split(jax.random.key(seed), 7)
    return {
        "image_emb": normal_values(arg_keys[0], (PAIRS, EMB), (EMB ** -0.5), 0.15625, ((0, 48), (1, 16)), jnp.float32),
        "text_emb": normal_values(arg_keys[1], (PAIRS, EMB), (EMB ** -0.5), 0.15625, ((0, 16), (1, 48)), jnp.float32),
        "vision_feat": normal_values(arg_keys[2], (PAIRS, VIS), 0.02, 0.125, ((0, 48), (1, 16))),
        "positive": jax.random.permutation(arg_keys[3], PAIRS).astype(jnp.int32),
        "logit_scale": jnp.clip(jax.random.uniform(arg_keys[4], (1,), jnp.float32, 5.0, 15.0), 5.0, 15.0),
        "logit_bias": jnp.clip(jax.random.uniform(arg_keys[5], (1,), jnp.float32, -3.0, -1.0), -3.0, -1.0),
    }


def reference(image_emb, text_emb, vision_feat, positive, logit_scale, logit_bias):
    scale = logit_scale[0]
    bias = logit_bias[0]
    blocks = image_emb.reshape(N_IMG, ROWS_IMG, EMB)
    matches = positive.reshape(N_IMG, ROWS_IMG)
    columns = jnp.arange(PAIRS, dtype=jnp.int32)

    def step(carry, item):
        image_block, match_block = item
        logits = scale * jnp.dot(image_block, text_emb.T, precision=lax.Precision.HIGHEST, preferred_element_type=jnp.float32) + bias
        sign = jnp.where(match_block[:, None] == columns[None, :], 1.0, -1.0).astype(jnp.float32)
        slope = -sign * jax.nn.sigmoid(-sign * logits)
        image_grad = scale * jnp.dot(slope, text_emb, precision=lax.Precision.HIGHEST, preferred_element_type=jnp.float32)
        carry = carry + scale * jnp.dot(slope.T, image_block, precision=lax.Precision.HIGHEST, preferred_element_type=jnp.float32)
        return carry, image_grad

    start = jnp.zeros((PAIRS, EMB), jnp.float32)
    grad_text, pieces = lax.scan(step, start, (blocks, matches))
    grad_image = pieces.reshape(PAIRS, EMB)
    image_low = grad_image.astype(jnp.bfloat16)
    grad_proj = jnp.dot(vision_feat.T, image_low, preferred_element_type=jnp.float32)
    return grad_image, grad_text, grad_proj
```

```python
import jax
import jax.numpy as jnp
from jax import lax
from jax.sharding import Mesh
from jax.sharding import PartitionSpec as P


IMG = ("yl", "z", "core")
TXT = ("x", "yh")
CHIPS = ("yl", "z")
HALF = jnp.float16
F32 = jnp.float32
HIGH = lax.Precision.HIGH

EMB_UP = 2.0**18
IMAGE_UP = 2.0**10
TEXT_UP = (2.0**11, 2.0**10, 2.0**9, 2.0**8, 2.0**7)
PROJ_UP = (2.0**-2, 2.0**-3)


def exchange(tiles, axis):
    return lax.all_to_all(tiles, axis, split_axis=0, concat_axis=0, tiled=True)


def to_all(array, axis):
    return exchange(jnp.broadcast_to(array[None], (lax.axis_size(axis), *array.shape)), axis)


def swap(array):
    return lax.ppermute(array, "core", ((0, 1), (1, 0)))


def shifted(array, axis, step):
    length = lax.axis_size(axis)
    return lax.ppermute(array, axis, tuple((i, (i + step) % length) for i in range(length)))


def in_order(came, place):
    length = len(came)
    return jnp.stack(
        [
            lax.select_n(place, *(came[(here - member) % length] for here in range(length)))
            for member in range(length)
        ]
    )


def per_device(image_emb, text_emb, vision_feat, positive, logit_scale, logit_bias):
    scale = logit_scale[0]
    bias = logit_bias[0]
    core = lax.axis_index("core")
    yl, z = lax.axis_index("yl"), lax.axis_index("z")

    def dot(a, b, ca, cb):
        return lax.dot_general(
            a, b, (((ca,), (cb,)), ((), ())), precision=HIGH, preferred_element_type=F32
        )

    def of_core(blocks, which):
        blocks = blocks.reshape(24, 2, 32, blocks.shape[-1])
        return lax.dynamic_index_in_dim(blocks, which, 1, keepdims=False).reshape(768, -1)

    text_tile = (text_emb.T * EMB_UP).astype(HALF)
    image_tile = (image_emb.T * EMB_UP).astype(HALF)
    own = to_all(text_tile, CHIPS)
    other = swap(own).reshape(768, -1).astype(F32)
    own = own.reshape(768, -1).astype(F32)
    near = jnp.stack([image_tile] + [shifted(image_tile, "yh", k) for k in (1, 2, 3)])
    far = [near] + [shifted(near, "x", k) for k in (1, 2, 3)]
    by_x = in_order(far, lax.axis_index("x"))
    image_full = in_order([by_x[:, k] for k in range(4)], lax.axis_index("yh"))
    image_full = jnp.moveaxis(image_full, 0, 1).astype(F32)
    image_own = of_core(image_full, core)
    image_other = of_core(image_full, 1 - core)

    text_rows = own.shape[1]
    first_col = lax.axis_index(TXT) * text_rows
    columns = first_col + lax.iota(jnp.int32, text_rows)
    products = dot(image_own, own, 0, 0) + dot(image_other, other, 0, 0)
    logits = (scale * (1.0 / EMB_UP**2)) * products + bias
    sign = jnp.where(positive[:, None] == columns[None, :], 1.0, -1.0).astype(F32)
    slope = -sign * jax.nn.sigmoid(-sign * logits)
    up = IMAGE_UP / EMB_UP
    first = (dot(own, slope, 1, 1) * up).astype(HALF).reshape(24, 32, -1)
    second = (dot(other, slope, 1, 1) * up).astype(HALF).reshape(24, 32, -1)
    sent = jnp.stack(
        (jnp.where(core == 0, first, second), jnp.where(core == 0, second, first)), axis=1
    )
    got = exchange(sent.reshape(16, 96, -1), TXT)
    grad_image = got.astype(F32).sum(axis=0) * (scale * (1.0 / IMAGE_UP))
    image_low = to_all(grad_image.astype(jnp.bfloat16), TXT)

    theirs = dot(image_other, slope, 1, 0)
    got = swap((theirs * (TEXT_UP[0] / EMB_UP)).astype(HALF))
    mine = dot(image_own, slope, 1, 0)
    tiles = mine * (1.0 / EMB_UP) + got.astype(F32) * (1.0 / TEXT_UP[0])
    tiles = tiles.reshape(2, 3, 2, 2, 32, text_rows)
    stages = (
        ("yl", yl, 0, ((0, 1), (1, 0))),
        ("z", z % 2, 2, tuple((i, i ^ 1) for i in range(12))),
        ("z", (z // 2) % 2, 1, tuple((i, i ^ 2) for i in range(12))),
    )
    for k, (axis, place, dim, pairs) in enumerate(stages, 1):
        theirs = lax.dynamic_index_in_dim(tiles, 1 - place, dim, keepdims=False)
        got = lax.ppermute((theirs * TEXT_UP[k]).astype(HALF), axis, pairs)
        mine = lax.dynamic_index_in_dim(tiles, place, dim, keepdims=False)
        tiles = mine + got.astype(F32) * (1.0 / TEXT_UP[k])
    block = z // 4
    total = lax.dynamic_index_in_dim(tiles, block, 0, keepdims=False)
    for step in (1, 2):
        theirs = lax.dynamic_index_in_dim(tiles, (block + step) % 3, 0, keepdims=False)
        got = shifted((theirs * TEXT_UP[4]).astype(HALF), "z", 4 * step)
        total = total + got.astype(F32) * (1.0 / TEXT_UP[4])
    grad_text = total * scale

    def weights(which):
        low = of_core(image_low, which)
        return lax.dot_general(low, vision_feat, (((1,), (0,)), ((), ())), preferred_element_type=F32)

    got = swap((weights(1 - core) * PROJ_UP[0]).astype(HALF))
    mine = weights(core)
    sent = ((mine + got.astype(F32) * (1.0 / PROJ_UP[0])) * PROJ_UP[1]).astype(HALF)
    got = exchange(sent.reshape(24, 32, -1), CHIPS)
    grad_proj = got.astype(F32).sum(axis=0) * (1.0 / PROJ_UP[1])
    return (grad_image.T, grad_text.T, grad_proj.T)


def solution(mesh):
    torus = Mesh(mesh.devices.reshape(2, 12, 2, 4, 4), (*IMG, *TXT))
    in_specs = (P(IMG, TXT), P(TXT, IMG), P(IMG, TXT), P(IMG), P(), P())
    out_specs = (P(IMG, TXT), P(TXT, IMG), P(TXT, IMG))
    return jax.shard_map(
        per_device, mesh=torus, in_specs=in_specs, out_specs=out_specs, check_vma=False
    )
```

```python
import jax
import jax.numpy as jnp
from jax import lax
from jax.sharding import Mesh
from jax.sharding import PartitionSpec as P


IMG = ("yl", "z", "core")
TXT = ("x", "yh")
CHIPS = ("yl", "z")
HALF = jnp.float16
F32 = jnp.float32
HIGH = lax.Precision.HIGH

EMB_UP = 2.0**18
IMAGE_UP = 2.0**10
TEXT_UP = (2.0**11, 2.0**10, 2.0**9, 2.0**7, 2.0**6)
PROJ_UP = (2.0**-2, 2.0**-3)


def exchange(tiles, axis):
    return lax.all_to_all(tiles, axis, split_axis=0, concat_axis=0, tiled=True)


def to_all(array, axis):
    return exchange(jnp.broadcast_to(array[None], (lax.axis_size(axis), *array.shape)), axis)


def swap(array):
    return lax.ppermute(array, "core", ((0, 1), (1, 0)))


def shifted(array, axis, step):
    length = lax.axis_size(axis)
    return lax.ppermute(array, axis, tuple((i, (i + step) % length) for i in range(length)))


def in_order(came, place):
    length = len(came)
    return jnp.stack(
        [
            lax.select_n(place, *(came[(here - member) % length] for here in range(length)))
            for member in range(length)
        ]
    )


def per_device(image_emb, text_emb, vision_feat, positive, logit_scale, logit_bias):
    scale = logit_scale[0]
    bias = logit_bias[0]
    core = lax.axis_index("core")
    yl, z = lax.axis_index("yl"), lax.axis_index("z")

    def dot(a, b, ca, cb):
        return lax.dot_general(
            a, b, (((ca,), (cb,)), ((), ())), precision=HIGH, preferred_element_type=F32
        )

    def of_core(blocks, which):
        blocks = blocks.reshape(24, 2, 32, blocks.shape[-1])
        return lax.dynamic_index_in_dim(blocks, which, 1, keepdims=False).reshape(768, -1)

    text_tile = (text_emb.T * EMB_UP).astype(HALF)
    image_tile = (image_emb.T * EMB_UP).astype(HALF)
    own = to_all(text_tile, CHIPS)
    other = swap(own).reshape(768, -1).astype(F32)
    own = own.reshape(768, -1).astype(F32)
    near = jnp.stack([image_tile] + [shifted(image_tile, "yh", k) for k in (1, 2, 3)])
    far = [near] + [shifted(near, "x", k) for k in (1, 3)]
    far.insert(2, shifted(near, "x", 2))
    by_x = in_order(far, lax.axis_index("x"))
    image_full = in_order([by_x[:, k] for k in range(4)], lax.axis_index("yh"))
    image_full = jnp.moveaxis(image_full, 0, 1).astype(F32)
    image_own = of_core(image_full, core)
    image_other = of_core(image_full, 1 - core)

    text_rows = own.shape[1]
    first_col = lax.axis_index(TXT) * text_rows
    columns = first_col + lax.iota(jnp.int32, text_rows)
    products = dot(image_own, own, 0, 0) + dot(image_other, other, 0, 0)
    logits = (scale * (1.0 / EMB_UP**2)) * products + bias
    sign = jnp.where(positive[:, None] == columns[None, :], 1.0, -1.0).astype(F32)
    slope = -sign * jax.nn.sigmoid(-sign * logits)
    up = IMAGE_UP / EMB_UP
    first = (dot(own, slope, 1, 1) * up).astype(HALF).reshape(24, 32, -1)
    second = (dot(other, slope, 1, 1) * up).astype(HALF).reshape(24, 32, -1)
    sent = jnp.stack(
        (jnp.where(core == 0, first, second), jnp.where(core == 0, second, first)), axis=1
    )
    got = exchange(sent.reshape(16, 96, -1), TXT)
    grad_image = got.astype(F32).sum(axis=0) * (scale * (1.0 / IMAGE_UP))
    image_low = to_all(grad_image.astype(jnp.bfloat16), TXT)

    theirs = dot(image_other, slope, 1, 0)
    got = swap((theirs * (TEXT_UP[0] / EMB_UP)).astype(HALF))
    mine = dot(image_own, slope, 1, 0)
    tiles = mine * (1.0 / EMB_UP) + got.astype(F32) * (1.0 / TEXT_UP[0])
    tiles = tiles.reshape(2, 3, 2, 2, 32, text_rows)

    def halve(tiles, k, axis, place, dim, pairs):
        theirs = lax.dynamic_index_in_dim(tiles, 1 - place, dim, keepdims=False)
        got = lax.ppermute((theirs * TEXT_UP[k]).astype(HALF), axis, pairs)
        mine = lax.dynamic_index_in_dim(tiles, place, dim, keepdims=False)
        return mine + got.astype(F32) * (1.0 / TEXT_UP[k])

    tiles = halve(tiles, 1, "yl", yl, 0, ((0, 1), (1, 0)))
    block = z // 4
    came = []
    for step in (1, 2):
        theirs = lax.dynamic_index_in_dim(tiles, (block + step) % 3, 0, keepdims=False)
        came.append(shifted((theirs * TEXT_UP[2]).astype(HALF), "z", 4 * step))
    tiles = lax.dynamic_index_in_dim(tiles, block, 0, keepdims=False)
    tiles = tiles + (came[0].astype(F32) + came[1].astype(F32)) * (1.0 / TEXT_UP[2])
    tiles = halve(tiles, 3, "z", z % 2, 1, tuple((i, i ^ 1) for i in range(12)))
    total = halve(tiles, 4, "z", (z // 2) % 2, 0, tuple((i, i ^ 2) for i in range(12)))
    grad_text = total * scale

    def weights(which):
        low = of_core(image_low, which).reshape(24, 32, -1)
        return lax.dot_general(low, vision_feat, (((2,), (0,)), ((), ())), preferred_element_type=F32)

    got = swap((weights(1 - core) * PROJ_UP[0]).astype(HALF))
    mine = weights(core)
    sent = ((mine + got.astype(F32) * (1.0 / PROJ_UP[0])) * PROJ_UP[1]).astype(HALF)
    got = exchange(sent, CHIPS)
    grad_proj = got.astype(F32).sum(axis=0) * (1.0 / PROJ_UP[1])
    return (grad_image.T, grad_text.T, grad_proj.T)


def solution(mesh):
    torus = Mesh(mesh.devices.reshape(2, 12, 2, 4, 4), (*IMG, *TXT))
    in_specs = (P(IMG, TXT), P(TXT, IMG), P(IMG, TXT), P(IMG), P(), P())
    out_specs = (P(IMG, TXT), P(TXT, IMG), P(TXT, IMG))
    return jax.shard_map(
        per_device, mesh=torus, in_specs=in_specs, out_specs=out_specs, check_vma=False
    )
```

```python
import jax
import jax.numpy as jnp
from jax import lax
from jax.sharding import Mesh
from jax.sharding import PartitionSpec as P


IMG = ("yl", "z", "core")
TXT = ("x", "yh")
CHIPS = ("yl", "z")
HALF = jnp.float16
F32 = jnp.float32
HIGH = lax.Precision.HIGH

EMB_UP = 2.0**18
IMAGE_UP = 2.0**10
TEXT_UP = (2.0**11, 2.0**10, 2.0**9, 2.0**7, 2.0**6)
PROJ_UP = (2.0**-2, 2.0**-3)


def exchange(tiles, axis):
    return lax.all_to_all(tiles, axis, split_axis=0, concat_axis=0, tiled=True)


def to_all(array, axis):
    return exchange(jnp.broadcast_to(array[None], (lax.axis_size(axis), *array.shape)), axis)


def swap(array):
    return lax.ppermute(array, "core", ((0, 1), (1, 0)))


def shifted(array, axis, step):
    length = lax.axis_size(axis)
    return lax.ppermute(array, axis, tuple((i, (i + step) % length) for i in range(length)))


def in_order(came, place):
    length = len(came)
    return jnp.stack(
        [
            lax.select_n(place, *(came[(here - member) % length] for here in range(length)))
            for member in range(length)
        ]
    )


def per_device(image_emb, text_emb, vision_feat, positive, logit_scale, logit_bias):
    scale = logit_scale[0]
    bias = logit_bias[0]
    core = lax.axis_index("core")
    yl, z = lax.axis_index("yl"), lax.axis_index("z")

    def dot(a, b, ca, cb):
        return lax.dot_general(
            a, b, (((ca,), (cb,)), ((), ())), precision=HIGH, preferred_element_type=F32
        )

    def of_core(blocks, which):
        blocks = blocks.reshape(24, 2, 32, blocks.shape[-1])
        return lax.dynamic_index_in_dim(blocks, which, 1, keepdims=False).reshape(768, -1)

    text_tile = (text_emb.T * EMB_UP).astype(HALF)
    image_tile = (image_emb.T * EMB_UP).astype(HALF)
    across = shifted(image_tile, "yh", 2)
    own = to_all(text_tile, CHIPS)
    other = swap(own).reshape(768, -1).astype(F32)
    own = own.reshape(768, -1).astype(F32)
    near = jnp.stack((image_tile, shifted(image_tile, "yh", 1), across, shifted(image_tile, "yh", 3)))
    far = [near] + [shifted(near, "x", k) for k in (1, 2, 3)]
    by_x = in_order(far, lax.axis_index("x"))
    image_full = in_order([by_x[:, k] for k in range(4)], lax.axis_index("yh"))
    image_full = jnp.moveaxis(image_full, 0, 1).astype(F32)
    image_own = of_core(image_full, core)
    image_other = of_core(image_full, 1 - core)

    text_rows = own.shape[1]
    first_col = lax.axis_index(TXT) * text_rows
    columns = first_col + lax.iota(jnp.int32, text_rows)
    products = dot(image_own, own, 0, 0) + dot(image_other, other, 0, 0)
    logits = (scale * (1.0 / EMB_UP**2)) * products + bias
    sign = jnp.where(positive[:, None] == columns[None, :], 1.0, -1.0).astype(F32)
    slope = -sign * jax.nn.sigmoid(-sign * logits)
    up = IMAGE_UP / EMB_UP
    first = (dot(own, slope, 1, 1) * up).astype(HALF).reshape(24, 32, -1)
    second = (dot(other, slope, 1, 1) * up).astype(HALF).reshape(24, 32, -1)
    sent = jnp.stack(
        (jnp.where(core == 0, first, second), jnp.where(core == 0, second, first)), axis=1
    )
    got = exchange(sent.reshape(16, 96, -1), TXT)
    grad_image = got.astype(F32).sum(axis=0) * (scale * (1.0 / IMAGE_UP))
    image_low = to_all(grad_image.astype(jnp.bfloat16), TXT)

    theirs = dot(image_other, slope, 1, 0)
    got = swap((theirs * (TEXT_UP[0] / EMB_UP)).astype(HALF))
    mine = dot(image_own, slope, 1, 0)
    tiles = mine * (1.0 / EMB_UP) + got.astype(F32) * (1.0 / TEXT_UP[0])
    tiles = tiles.reshape(2, 3, 2, 2, 32, text_rows)

    def halve(tiles, k, axis, place, dim, pairs):
        theirs = lax.dynamic_index_in_dim(tiles, 1 - place, dim, keepdims=False)
        got = lax.ppermute((theirs * TEXT_UP[k]).astype(HALF), axis, pairs)
        mine = lax.dynamic_index_in_dim(tiles, place, dim, keepdims=False)
        return mine + got.astype(F32) * (1.0 / TEXT_UP[k])

    tiles = halve(tiles, 1, "yl", yl, 0, ((0, 1), (1, 0)))
    block = z // 4
    came = []
    for step in (1, 2):
        theirs = lax.dynamic_index_in_dim(tiles, (block + step) % 3, 0, keepdims=False)
        came.append(shifted((theirs * TEXT_UP[2]).astype(HALF), "z", 4 * step))
    tiles = lax.dynamic_index_in_dim(tiles, block, 0, keepdims=False)
    tiles = tiles + (came[0].astype(F32) + came[1].astype(F32)) * (1.0 / TEXT_UP[2])
    tiles = halve(tiles, 3, "z", z % 2, 1, tuple((i, i ^ 1) for i in range(12)))
    total = halve(tiles, 4, "z", (z // 2) % 2, 0, tuple((i, i ^ 2) for i in range(12)))
    grad_text = total * scale

    def weights(which):
        low = of_core(image_low, which).reshape(24, 32, -1)
        return lax.dot_general(low, vision_feat, (((2,), (0,)), ((), ())), preferred_element_type=F32)

    got = swap((weights(1 - core) * PROJ_UP[0]).astype(HALF))
    mine = weights(core)
    sent = ((mine + got.astype(F32) * (1.0 / PROJ_UP[0])) * PROJ_UP[1]).astype(HALF)
    end = jnp.concatenate((sent[:, :16, 256:], sent[:, 16:, 256:]), axis=2)
    sent = jnp.concatenate((sent[:, :, :128], sent[:, :, 128:256], end), axis=1)
    got = exchange(sent, CHIPS)
    total = got.astype(F32).sum(axis=0) * (1.0 / PROJ_UP[1])
    end = jnp.concatenate((total[64:, :64], total[64:, 64:]), axis=0)
    grad_proj = jnp.concatenate((total[:32], total[32:64], end), axis=1)
    return (grad_image.T, grad_text.T, grad_proj.T)


def solution(mesh):
    torus = Mesh(mesh.devices.reshape(2, 12, 2, 4, 4), (*IMG, *TXT))
    in_specs = (P(IMG, TXT), P(TXT, IMG), P(IMG, TXT), P(IMG), P(), P())
    out_specs = (P(IMG, TXT), P(TXT, IMG), P(TXT, IMG))
    return jax.shard_map(
        per_device, mesh=torus, in_specs=in_specs, out_specs=out_specs, check_vma=False
    )
```

```python
import jax
import jax.numpy as jnp
from jax import lax
from jax.sharding import Mesh
from jax.sharding import PartitionSpec as P


IMG = ("yl", "z", "core")
TXT = ("x", "yh")
CHIPS = ("yl", "z")
HALF = jnp.float16
F32 = jnp.float32
HIGH = lax.Precision.HIGH

EMB_UP = 2.0**18
IMAGE_UP = 2.0**10
TEXT_UP = (2.0**11, 2.0**10, 2.0**9, 2.0**8, 2.0**7)
PROJ_UP = (2.0**-2, 2.0**-3)


def exchange(tiles, axis):
    return lax.all_to_all(tiles, axis, split_axis=0, concat_axis=0, tiled=True)


def to_all(array, axis):
    return exchange(jnp.broadcast_to(array[None], (lax.axis_size(axis), *array.shape)), axis)


def swap(array):
    return lax.ppermute(array, "core", ((0, 1), (1, 0)))


def shifted(array, axis, step):
    length = lax.axis_size(axis)
    return lax.ppermute(array, axis, tuple((i, (i + step) % length) for i in range(length)))


def in_order(came, place):
    length = len(came)
    return jnp.stack(
        [
            lax.select_n(place, *(came[(here - member) % length] for here in range(length)))
            for member in range(length)
        ]
    )


def per_device(image_emb, text_emb, vision_feat, positive, logit_scale, logit_bias):
    scale = logit_scale[0]
    bias = logit_bias[0]
    core = lax.axis_index("core")
    yl, z = lax.axis_index("yl"), lax.axis_index("z")

    def dot(a, b, ca, cb):
        return lax.dot_general(
            a, b, (((ca,), (cb,)), ((), ())), precision=HIGH, preferred_element_type=F32
        )

    def of_core(blocks, which):
        blocks = blocks.reshape(24, 2, 32, blocks.shape[-1])
        return lax.dynamic_index_in_dim(blocks, which, 1, keepdims=False).reshape(768, -1)

    text_tile = (text_emb.T * EMB_UP).astype(HALF)
    image_tile = (image_emb.T * EMB_UP).astype(HALF)
    own = to_all(text_tile, CHIPS)
    other = swap(own).reshape(768, -1).astype(F32)
    own = own.reshape(768, -1).astype(F32)
    near = jnp.stack([image_tile] + [shifted(image_tile, "yh", k) for k in (1, 2, 3)])
    far = [near] + [shifted(near, "x", k) for k in (1, 2, 3)]
    by_x = in_order(far, lax.axis_index("x"))
    image_full = in_order([by_x[:, k] for k in range(4)], lax.axis_index("yh"))
    image_full = jnp.moveaxis(image_full, 0, 1).astype(F32)
    image_own = of_core(image_full, core)
    image_other = of_core(image_full, 1 - core)

    text_rows = own.shape[1]
    first_col = lax.axis_index(TXT) * text_rows
    columns = first_col + lax.iota(jnp.int32, text_rows)
    products = dot(image_own, own, 0, 0) + dot(image_other, other, 0, 0)
    logits = (scale * (1.0 / EMB_UP**2)) * products + bias
    sign = jnp.where(positive[:, None] == columns[None, :], 1.0, -1.0).astype(F32)
    slope = -sign * jax.nn.sigmoid(-sign * logits)
    up = IMAGE_UP / EMB_UP
    first = (dot(own, slope, 1, 1) * up).astype(HALF).reshape(24, 32, -1)
    second = (dot(other, slope, 1, 1) * up).astype(HALF).reshape(24, 32, -1)
    sent = jnp.stack(
        (jnp.where(core == 0, first, second), jnp.where(core == 0, second, first)), axis=1
    )
    got = exchange(sent.reshape(16, 96, -1), TXT)
    grad_image = got.astype(F32).sum(axis=0) * (scale * (1.0 / IMAGE_UP))
    image_low = to_all(grad_image.astype(jnp.bfloat16), TXT)

    theirs = dot(image_other, slope, 1, 0)
    got = swap((theirs * (TEXT_UP[0] / EMB_UP)).astype(HALF))
    mine = dot(image_own, slope, 1, 0)
    tiles = mine * (1.0 / EMB_UP) + got.astype(F32) * (1.0 / TEXT_UP[0])
    tiles = tiles.reshape(2, 3, 2, 2, 32, text_rows)

    def halve(tiles, k, axis, place, dim, pairs):
        theirs = lax.dynamic_index_in_dim(tiles, 1 - place, dim, keepdims=False)
        got = lax.ppermute((theirs * TEXT_UP[k]).astype(HALF), axis, pairs)
        mine = lax.dynamic_index_in_dim(tiles, place, dim, keepdims=False)
        return mine + got.astype(F32) * (1.0 / TEXT_UP[k])

    tiles = halve(tiles, 1, "yl", yl, 0, ((0, 1), (1, 0)))
    tiles = halve(tiles, 2, "z", z % 2, 2, tuple((i, i ^ 1) for i in range(12)))
    tiles = halve(tiles, 3, "z", (z // 2) % 2, 1, tuple((i, i ^ 2) for i in range(12)))
    block = z // 4
    came = []
    for step in (1, 2):
        theirs = lax.dynamic_index_in_dim(tiles, (block + step) % 3, 0, keepdims=False)
        came.append(shifted((theirs * TEXT_UP[4]).astype(HALF), "z", 4 * step))
    total = lax.dynamic_index_in_dim(tiles, block, 0, keepdims=False)
    total = total + (came[0].astype(F32) + came[1].astype(F32)) * (1.0 / TEXT_UP[4])
    grad_text = total * scale

    def weights(which):
        low = of_core(image_low, which).reshape(24, 32, -1)
        return lax.dot_general(low, vision_feat, (((2,), (0,)), ((), ())), preferred_element_type=F32)

    got = swap((weights(1 - core) * PROJ_UP[0]).astype(HALF))
    mine = weights(core)
    sent = ((mine + got.astype(F32) * (1.0 / PROJ_UP[0])) * PROJ_UP[1]).astype(HALF)
    end = jnp.concatenate((sent[:, :16, 256:], sent[:, 16:, 256:]), axis=2)
    sent = jnp.concatenate((sent[:, :, :128], sent[:, :, 128:256], end), axis=1)
    got = exchange(sent, CHIPS)
    total = got.astype(F32).sum(axis=0) * (1.0 / PROJ_UP[1])
    end = jnp.concatenate((total[64:, :64], total[64:, 64:]), axis=0)
    grad_proj = jnp.concatenate((total[:32], total[32:64], end), axis=1)
    return (grad_image.T, grad_text.T, grad_proj.T)


def solution(mesh):
    torus = Mesh(mesh.devices.reshape(2, 12, 2, 4, 4), (*IMG, *TXT))
    in_specs = (P(IMG, TXT), P(TXT, IMG), P(IMG, TXT), P(IMG), P(), P())
    out_specs = (P(IMG, TXT), P(TXT, IMG), P(TXT, IMG))
    return jax.shard_map(
        per_device, mesh=torus, in_specs=in_specs, out_specs=out_specs, check_vma=False
    )
```

```python
import jax
import jax.numpy as jnp
from jax import lax
from jax.sharding import Mesh
from jax.sharding import PartitionSpec as P


IMG = ("yl", "z", "core")
TXT = ("x", "yh")
CHIPS = ("yl", "z")
HALF = jnp.float16
F32 = jnp.float32
HIGH = lax.Precision.HIGH

EMB_UP = 2.0**18
IMAGE_UP = 2.0**10
TEXT_UP = (2.0**11, 2.0**10, 2.0**9, 2.0**8, 2.0**6)
PROJ_UP = (2.0**-2, 2.0**-3)


def exchange(tiles, axis):
    return lax.all_to_all(tiles, axis, split_axis=0, concat_axis=0, tiled=True)


def to_all(array, axis):
    return exchange(jnp.broadcast_to(array[None], (lax.axis_size(axis), *array.shape)), axis)


def swap(array):
    return lax.ppermute(array, "core", ((0, 1), (1, 0)))


def shifted(array, axis, step):
    length = lax.axis_size(axis)
    return lax.ppermute(array, axis, tuple((i, (i + step) % length) for i in range(length)))


def in_order(came, place):
    length = len(came)
    return jnp.stack(
        [
            lax.select_n(place, *(came[(here - member) % length] for here in range(length)))
            for member in range(length)
        ]
    )


def per_device(image_emb, text_emb, vision_feat, positive, logit_scale, logit_bias):
    scale = logit_scale[0]
    bias = logit_bias[0]
    core = lax.axis_index("core")
    yl, z = lax.axis_index("yl"), lax.axis_index("z")

    def dot(a, b, ca, cb):
        return lax.dot_general(
            a, b, (((ca,), (cb,)), ((), ())), precision=HIGH, preferred_element_type=F32
        )

    def of_core(blocks, which):
        blocks = blocks.reshape(24, 2, 32, blocks.shape[-1])
        return lax.dynamic_index_in_dim(blocks, which, 1, keepdims=False).reshape(768, -1)

    text_tile = (text_emb.T * EMB_UP).astype(HALF)
    image_tile = (image_emb.T * EMB_UP).astype(HALF)
    own = to_all(text_tile, CHIPS)
    other = swap(own).reshape(768, -1).astype(F32)
    own = own.reshape(768, -1).astype(F32)
    near = jnp.stack([image_tile] + [shifted(image_tile, "yh", k) for k in (1, 2, 3)])
    far = [near] + [shifted(near, "x", k) for k in (1, 2, 3)]
    by_x = in_order(far, lax.axis_index("x"))
    image_full = in_order([by_x[:, k] for k in range(4)], lax.axis_index("yh"))
    image_full = jnp.moveaxis(image_full, 0, 1).astype(F32)
    image_own = of_core(image_full, core)
    image_other = of_core(image_full, 1 - core)

    text_rows = own.shape[1]
    first_col = lax.axis_index(TXT) * text_rows
    columns = first_col + lax.iota(jnp.int32, text_rows)
    products = dot(image_own, own, 0, 0) + dot(image_other, other, 0, 0)
    logits = (scale * (1.0 / EMB_UP**2)) * products + bias
    sign = jnp.where(positive[:, None] == columns[None, :], 1.0, -1.0).astype(F32)
    slope = -sign * jax.nn.sigmoid(-sign * logits)
    up = IMAGE_UP / EMB_UP
    first = (dot(own, slope, 1, 1) * up).astype(HALF).reshape(24, 32, -1)
    second = (dot(other, slope, 1, 1) * up).astype(HALF).reshape(24, 32, -1)
    sent = jnp.stack(
        (jnp.where(core == 0, first, second), jnp.where(core == 0, second, first)), axis=1
    )
    got = exchange(sent.reshape(16, 96, -1), TXT)
    grad_image = got.astype(F32).sum(axis=0) * (scale * (1.0 / IMAGE_UP))
    image_low = to_all(grad_image.astype(jnp.bfloat16), TXT)

    theirs = dot(image_other, slope, 1, 0)
    got = swap((theirs * (TEXT_UP[0] / EMB_UP)).astype(HALF))
    mine = dot(image_own, slope, 1, 0)
    tiles = mine * (1.0 / EMB_UP) + got.astype(F32) * (1.0 / TEXT_UP[0])
    tiles = tiles.reshape(2, 3, 2, 2, 32, text_rows)

    def halve(tiles, k, axis, place, dim, pairs):
        theirs = lax.dynamic_index_in_dim(tiles, 1 - place, dim, keepdims=False)
        got = lax.ppermute((theirs * TEXT_UP[k]).astype(HALF), axis, pairs)
        mine = lax.dynamic_index_in_dim(tiles, place, dim, keepdims=False)
        return mine + got.astype(F32) * (1.0 / TEXT_UP[k])

    tiles = halve(tiles, 1, "yl", yl, 0, ((0, 1), (1, 0)))
    tiles = halve(tiles, 2, "z", z % 2, 2, tuple((i, i ^ 1) for i in range(12)))
    block = z // 4
    came = []
    for step in (1, 2):
        theirs = lax.dynamic_index_in_dim(tiles, (block + step) % 3, 0, keepdims=False)
        came.append(shifted((theirs * TEXT_UP[3]).astype(HALF), "z", 4 * step))
    tiles = lax.dynamic_index_in_dim(tiles, block, 0, keepdims=False)
    tiles = tiles + (came[0].astype(F32) + came[1].astype(F32)) * (1.0 / TEXT_UP[3])
    total = halve(tiles, 4, "z", (z // 2) % 2, 0, tuple((i, i ^ 2) for i in range(12)))
    grad_text = total * scale

    def weights(which):
        low = of_core(image_low, which).reshape(24, 32, -1)
        return lax.dot_general(low, vision_feat, (((2,), (0,)), ((), ())), preferred_element_type=F32)

    got = swap((weights(1 - core) * PROJ_UP[0]).astype(HALF))
    mine = weights(core)
    sent = ((mine + got.astype(F32) * (1.0 / PROJ_UP[0])) * PROJ_UP[1]).astype(HALF)
    got = exchange(sent, CHIPS)
    grad_proj = got.astype(F32).sum(axis=0) * (1.0 / PROJ_UP[1])
    return (grad_image.T, grad_text.T, grad_proj.T)


def solution(mesh):
    torus = Mesh(mesh.devices.reshape(2, 12, 2, 4, 4), (*IMG, *TXT))
    in_specs = (P(IMG, TXT), P(TXT, IMG), P(IMG, TXT), P(IMG), P(), P())
    out_specs = (P(IMG, TXT), P(TXT, IMG), P(TXT, IMG))
    return jax.shard_map(
        per_device, mesh=torus, in_specs=in_specs, out_specs=out_specs, check_vma=False
    )
```

```python
import jax
import jax.numpy as jnp
from jax import lax
from jax.sharding import Mesh
from jax.sharding import PartitionSpec as P


IMG = ("yl", "z", "core")
TXT = ("x", "yh")
CHIPS = ("yl", "z")
HALF = jnp.float16
F32 = jnp.float32
HIGH = lax.Precision.HIGH

EMB_UP = 2.0**18
IMAGE_UP = 2.0**10
TEXT_UP = (2.0**11, 2.0**10, 2.0**9, 2.0**8, 2.0**7)
PROJ_UP = (2.0**-2, 2.0**-3)


def exchange(tiles, axis):
    return lax.all_to_all(tiles, axis, split_axis=0, concat_axis=0, tiled=True)


def to_all(array, axis):
    return exchange(jnp.broadcast_to(array[None], (lax.axis_size(axis), *array.shape)), axis)


def swap(array):
    return lax.ppermute(array, "core", ((0, 1), (1, 0)))


def shifted(array, axis, step):
    length = lax.axis_size(axis)
    return lax.ppermute(array, axis, tuple((i, (i + step) % length) for i in range(length)))


def in_order(came, place):
    length = len(came)
    return jnp.stack(
        [
            lax.select_n(place, *(came[(here - member) % length] for here in range(length)))
            for member in range(length)
        ]
    )


def per_device(image_emb, text_emb, vision_feat, positive, logit_scale, logit_bias):
    scale = logit_scale[0]
    bias = logit_bias[0]
    core = lax.axis_index("core")
    yl, z = lax.axis_index("yl"), lax.axis_index("z")

    def dot(a, b, ca, cb):
        return lax.dot_general(
            a, b, (((ca,), (cb,)), ((), ())), precision=HIGH, preferred_element_type=F32
        )

    def of_core(blocks, which):
        blocks = blocks.reshape(24, 2, 32, blocks.shape[-1])
        return lax.dynamic_index_in_dim(blocks, which, 1, keepdims=False).reshape(768, -1)

    text_tile = (text_emb.T * EMB_UP).astype(HALF)
    image_tile = (image_emb.T * EMB_UP).astype(HALF)
    own = to_all(text_tile, CHIPS)
    other = swap(own).reshape(768, -1).astype(F32)
    own = own.reshape(768, -1).astype(F32)
    near = jnp.stack([image_tile] + [shifted(image_tile, "yh", k) for k in (1, 2, 3)])
    far = [near] + [shifted(near, "x", k) for k in (1, 2, 3)]
    by_x = in_order(far, lax.axis_index("x"))
    image_full = in_order([by_x[:, k] for k in range(4)], lax.axis_index("yh"))
    image_full = jnp.moveaxis(image_full, 0, 1).astype(F32)
    image_own = of_core(image_full, core)
    image_other = of_core(image_full, 1 - core)

    text_rows = own.shape[1]
    first_col = lax.axis_index(TXT) * text_rows
    columns = first_col + lax.iota(jnp.int32, text_rows)
    products = dot(image_own, own, 0, 0) + dot(image_other, other, 0, 0)
    logits = (scale * (1.0 / EMB_UP**2)) * products + bias
    sign = jnp.where(positive[:, None] == columns[None, :], 1.0, -1.0).astype(F32)
    slope = -sign * jax.nn.sigmoid(-sign * logits)
    up = IMAGE_UP / EMB_UP
    first = (dot(own, slope, 1, 1) * up).astype(HALF).reshape(24, 32, -1)
    second = (dot(other, slope, 1, 1) * up).astype(HALF).reshape(24, 32, -1)
    sent = jnp.stack(
        (jnp.where(core == 0, first, second), jnp.where(core == 0, second, first)), axis=1
    )
    got = exchange(sent.reshape(16, 96, -1), TXT)
    grad_image = got.astype(F32).sum(axis=0) * (scale * (1.0 / IMAGE_UP))
    image_low = to_all(grad_image.astype(jnp.bfloat16), TXT)

    theirs = dot(image_other, slope, 1, 0)
    got = swap((theirs * (TEXT_UP[0] / EMB_UP)).astype(HALF))
    mine = dot(image_own, slope, 1, 0)
    tiles = mine * (1.0 / EMB_UP) + got.astype(F32) * (1.0 / TEXT_UP[0])
    tiles = tiles.reshape(2, 3, 2, 2, 32, text_rows)

    def halve(tiles, k, axis, place, dim, pairs):
        theirs = lax.dynamic_index_in_dim(tiles, 1 - place, dim, keepdims=False)
        got = lax.ppermute((theirs * TEXT_UP[k]).astype(HALF), axis, pairs)
        mine = lax.dynamic_index_in_dim(tiles, place, dim, keepdims=False)
        return mine + got.astype(F32) * (1.0 / TEXT_UP[k])

    tiles = halve(tiles, 1, "yl", yl, 0, ((0, 1), (1, 0)))
    tiles = halve(tiles, 2, "z", z % 2, 2, tuple((i, i ^ 1) for i in range(12)))
    tiles = halve(tiles, 3, "z", (z // 2) % 2, 1, tuple((i, i ^ 2) for i in range(12)))
    block = z // 4
    came = []
    for step in (1, 2):
        theirs = lax.dynamic_index_in_dim(tiles, (block + step) % 3, 0, keepdims=False)
        came.append(shifted((theirs * TEXT_UP[4]).astype(HALF), "z", 4 * step))
    total = lax.dynamic_index_in_dim(tiles, block, 0, keepdims=False)
    total = total + (came[0].astype(F32) + came[1].astype(F32)) * (1.0 / TEXT_UP[4])
    grad_text = total * scale

    def weights(which):
        low = of_core(image_low, which).reshape(24, 32, -1)
        return lax.dot_general(low, vision_feat, (((2,), (0,)), ((), ())), preferred_element_type=F32)

    got = swap((weights(1 - core) * PROJ_UP[0]).astype(HALF))
    mine = weights(core)
    sent = ((mine + got.astype(F32) * (1.0 / PROJ_UP[0])) * PROJ_UP[1]).astype(HALF)
    got = exchange(sent, CHIPS)
    grad_proj = got.astype(F32).sum(axis=0) * (1.0 / PROJ_UP[1])
    return (grad_image.T, grad_text.T, grad_proj.T)


def solution(mesh):
    torus = Mesh(mesh.devices.reshape(2, 12, 2, 4, 4), (*IMG, *TXT))
    in_specs = (P(IMG, TXT), P(TXT, IMG), P(IMG, TXT), P(IMG), P(), P())
    out_specs = (P(IMG, TXT), P(TXT, IMG), P(TXT, IMG))
    return jax.shard_map(
        per_device, mesh=torus, in_specs=in_specs, out_specs=out_specs, check_vma=False
    )
```
